32 devices in a mesh: blk: 4 (over y, x), grp: 8 (over z, core).
Axes of the slice: x: 2, y: 2, z: 4, core: 2. Of those that a mesh axis runs over, the one named last changes fastest.
Arguments:
- gradients: bfloat16 [8, 4, 851968], P('grp', 'blk'), may hold values from -48 to 48
- master: float32 [851968], P(('blk', 'grp')), may hold values from -0.06 to 0.06
- moment: float32 [851968], P(('blk', 'grp')), may hold values from -0.12 to 0.12
- second: float32 [851968], P(('blk', 'grp')), may hold values from 0.004 to 0.5
Outputs:
- weights: bfloat16 [851968], replicated
- master_new: float32 [851968], P(('blk', 'grp'))
- moment_new: float32 [851968], P(('blk', 'grp'))
- second_new: float32 [851968], P(('blk', 'grp'))
The draws below stay inside these ranges and needn't reach their ends.
All inputs are finite; a program needn't handle non-finite values.
Results may differ from the reference program's by a relative error of at most 0.015.
Values may be sent and summed in bfloat16 or wider, within the bound.
No kernel may reach another device: no remote copies, remote signals or barrier semaphores. Data moves between devices by JAX's collectives and lax.ppermute only.
A program may use at most 64 MiB of HBM per device.

```python
import math
import jax
import jax.numpy as jnp
from jax import lax

F = 6656
ROWS = 128
STEP = 8
ENTRIES = 851968
N_BLK = 4
N_GRP = 8


def draw_gradients(key, part):
    spread = 2.0 * N_BLK
    limit = 12.0 * N_BLK
    blocks = N_GRP * N_BLK
    width = ENTRIES // blocks
    noise_key = jax.random.fold_in(key, 11)
    pair_key = jax.random.fold_in(key, 12)
    target = jax.random.permutation(pair_key, blocks).reshape(N_GRP, N_BLK)
    marked = target[:, :, None] == jnp.arange(blocks)[None, None, :]
    factor = jnp.where(marked, 3.0, 1.0).astype(jnp.float32)[:, :, :, None]
    noise = jax.random.normal(noise_key, (N_GRP, N_BLK, blocks, width), jnp.float32) * spread
    values = jnp.clip(noise * factor, -limit, limit)
    return values.reshape(N_GRP, N_BLK, ENTRIES).astype(jnp.bfloat16)


def block_levels(stream_key, shape, split, low, high):
    def one(dim, parts):
        steps = jax.random.uniform(jax.random.fold_in(jax.random.fold_in(stream_key, 6), dim), (parts,), jnp.float32, low / len(split), high / len(split))
        return jnp.repeat(jnp.exp(steps), shape[dim] // parts).reshape((-1,) + (1,) * (len(shape) - dim - 1))

    level = one(*split[0])
    for cut in split[1:]:
        level = level * one(*cut)
    return level


def normal_values(stream_key, shape, scale, reach, pieces=(), dtype=jnp.bfloat16):
    result = scale * jax.random.normal(stream_key, shape, jnp.float32)
    if pieces:
        result = result * block_levels(stream_key, shape, pieces, -0.22, 0.18)
    return jnp.clip(result, -reach, reach).astype(dtype)


def setup_inputs(seed: int = 0) -> dict:
    key_of = jax.random.split(jax.random.key(seed), 5)
    return {
        "gradients": draw_gradients(jax.random.fold_in(key_of[4], 71), 0),
        "master": jnp.clip(jax.random.uniform(key_of[1], (ENTRIES,), jnp.float32, -0.06, 0.06) * block_levels(key_of[1], (ENTRIES,), ((0, 32),), -0.4, 0.0), -0.06, 0.06),
        "moment": normal_values(key_of[2], (ENTRIES,), 0.03, 0.12, ((0, 32),), jnp.float32),
        "second": jnp.clip(jnp.exp(math.log(0.5) - 4.828314 * jax.random.uniform(key_of[3], (ENTRIES,), jnp.float32) ** block_levels(key_of[3], (ENTRIES,), ((0, 32),), -0.2, 0.2)), 0.004, 0.5),
    }


def reference(gradients, master, moment, second):

    def accumulate(total, block):
        return (total + lax.optimization_barrier(jnp.sum(block.astype(jnp.float32), axis=0)), None)
    total, unused = lax.scan(accumulate, jnp.zeros((ROWS * F,), jnp.float32), gradients)
    grad = total / (N_BLK * N_GRP)
    moment_new = 0.9 * moment + 0.1 * grad
    second_new = 0.95 * second + 0.05 * grad * grad
    update = moment_new / (1.0 - 0.9 ** STEP) / (jnp.sqrt(second_new / (1.0 - 0.95 ** STEP)) + 1e-08)
    master_new = master - 0.03 * (update + 0.1 * master)
    weights = master_new.astype(jnp.bfloat16)
    return (weights, master_new, moment_new, second_new)
```

```python
import functools
import jax
import jax.numpy as jnp
from jax import lax
from jax.experimental import pallas as pl
from jax.experimental.pallas import tpu as pltpu
from jax.sharding import PartitionSpec as P

STEP = 8
AXES = ("blk", "grp")
F32, BF16 = jnp.float32, jnp.bfloat16


def own_slice(n_grp):
    return lax.axis_index("blk") * n_grp + lax.axis_index("grp")


def span(masks):
    out = [0]
    for m in masks:
        out += [m ^ o for o in out]
    return out


def pack_kernel(n_grp, width, masks, g_ref, *refs):
    outs, (held, sem) = refs[:-2], refs[-2:]
    core = lax.rem(lax.axis_index("grp"), 2)
    own = own_slice(n_grp)
    flat = [pair for group in masks for pair in group]

    def copy(i):
        even, odd = flat[i]
        at = jnp.bitwise_xor(own, jnp.where(core == 0, even, odd)) * width
        return pltpu.make_async_copy(g_ref.at[:, :, pl.ds(pl.multiple_of(at, width), width)], held.at[i], sem.at[i])

    for i in range(len(flat)):
        copy(i).start()
    i = 0
    for out, group in zip(outs, masks):
        for k in range(len(group)):
            copy(i).wait()
            out[k] = held[i, 0].reshape(out.shape[1:])
            i += 1


def pack(g, n_grp, width, masks):
    count = sum(len(group) for group in masks)
    rows = (width // 128, 128)
    return pl.pallas_call(
        functools.partial(pack_kernel, n_grp, width, masks),
        in_specs=[pl.BlockSpec(memory_space=pl.ANY)],
        out_specs=[pl.BlockSpec(memory_space=pltpu.VMEM)] * len(masks),
        out_shape=[jax.ShapeDtypeStruct((len(group),) + rows, BF16) for group in masks],
        scratch_shapes=[pltpu.VMEM((count, 1, 1, width), BF16), pltpu.SemaphoreType.DMA((count,))],
        cost_estimate=pl.CostEstimate(flops=0, bytes_accessed=6 * count * width, transcendentals=0),
    )(g)


def place_kernel(n_grp, n_parts, *refs):
    parts, out, sem = refs[:n_parts], refs[n_parts], refs[n_parts + 1]
    core = lax.rem(lax.axis_index("grp"), 2)
    own = own_slice(n_grp)
    return parts, out, sem, core, own


def place_body(n_grp, masks, *refs):
    parts, out, sem, core, own = place_kernel(n_grp, len(masks), *refs)
    copies = []
    for part, group in zip(parts, masks):
        for k, (even, odd) in enumerate(group):
            at = jnp.bitwise_xor(own, jnp.where(core == 0, even, odd))
            copies.append(pltpu.make_async_copy(part.at[k], out.at[at], sem.at[len(copies)]))
            copies[-1].start()
    for copy in copies:
        copy.wait()


def place(parts, n_grp, n_slices, masks):
    count = sum(len(group) for group in masks)
    rows = parts[0].shape[1:]
    return pl.pallas_call(
        functools.partial(place_body, n_grp, masks),
        in_specs=[pl.BlockSpec(memory_space=pltpu.VMEM)] * len(parts),
        out_specs=pl.BlockSpec(memory_space=pl.ANY),
        out_shape=jax.ShapeDtypeStruct((n_slices,) + rows, BF16),
        scratch_shapes=[pltpu.SemaphoreType.DMA((count,))],
    )(*parts)


def shards(n_blk, n_grp, gradients, master, moment, second):
    n_slices, n_z = n_blk * n_grp, n_grp // 2
    width = master.shape[0]
    tiled = width % 2048 == 0
    rows = (width // 128, 128) if tiled else (width,)

    bits = [1 << i for i in range(n_blk.bit_length() - 1)]
    order = (bits, bits[::-1])

    def move(value, mask_of):
        pairs = [(s, s ^ mask_of[s % 2]) for s in range(n_slices)]
        return lax.ppermute(value, AXES, pairs)

    def blk_mask(combo):
        return tuple(sum(order[c][i] for i in range(len(bits)) if combo >> i & 1) * n_grp for c in range(2))

    def pieces(combos, core_mask):
        out = []
        for combo in combos:
            even, odd = blk_mask(combo)
            if core_mask:
                even, odd = odd, even
            out += [(even ^ 2 * k ^ core_mask, odd ^ 2 * k ^ core_mask) for k in range(n_z)]
        return out

    own = own_slice(n_grp)
    core = lax.rem(own, 2)

    def take(masks):
        table = jnp.where(core == 0, jnp.array([m[0] for m in masks]), jnp.array([m[1] for m in masks]))
        return gradients.reshape(n_slices, width)[jnp.bitwise_xor(own, table)]

    def packed(groups):
        if tiled:
            return pack(gradients, n_grp, width, groups)
        return [take(group) for group in groups]

    n_stage = len(bits)
    half = 1 << max(n_stage - 1, 0)
    first = [2 * i + 1 for i in range(half)][::-1] if n_stage else [0]
    rest = [2 * i for i in range(half)][::-1] if n_stage else []

    (send_a,) = packed([pieces(first, 1)])
    got_a = move(send_a, (1, 1))
    own_a, send_b = packed([pieces(first, 0), pieces(rest, 1)])
    got_b = move(send_b, (1, 1))
    (own_b,) = packed([pieces(rest, 0)])

    total = {}
    for combos, mine, got in ((first, own_a, got_a), (rest, own_b, got_b)):
        for i, combo in enumerate(combos):
            at = slice(i * n_z, (i + 1) * n_z)
            total[combo] = mine[at].astype(F32) + got[at].astype(F32)

    for stage in range(n_stage):
        bit = 1 << stage
        left = [c for c in total if not c & bit]
        for urgent in (True, False):
            for combo in [c for c in left if bool(c & 2 * bit) == urgent]:
                got = move(total[combo | bit].astype(BF16), blk_mask(bit))
                total[combo] = total[combo] + got.astype(F32)
        total = {c: total[c] for c in left}
    part = total[0]

    radix = n_z
    while radix > 1:
        step = min(radix, 4)
        radix //= step
        part = part.reshape((step, radix) + rows)
        out = part[0]
        for k in reversed(range(1, step)):
            out = out + move(part[k].astype(BF16), (2 * k * radix,) * 2).astype(F32)
        part = out
    sums = part.reshape(rows)

    master, moment, second = (v.reshape(rows) for v in (master, moment, second))
    grad = sums / n_slices
    moment_new = 0.9 * moment + 0.1 * grad
    second_new = 0.95 * second + 0.05 * grad * grad
    update = moment_new / (1.0 - 0.9**STEP) / (jnp.sqrt(second_new / (1.0 - 0.95**STEP)) + 1e-08)
    master_new = master - 0.03 * (update + 0.1 * master)
    mine = master_new.astype(BF16)[None]

    radix = 1
    while radix < n_z:
        step = min(n_z // radix, 4)
        others = {k: move(mine, (2 * k * radix,) * 2) for k in reversed(range(1, step))}
        mine = jnp.concatenate([mine] + [others[k] for k in range(1, step)])
        radix *= step

    held = {0: mine}
    for stage in reversed(range(n_stage)):
        bit = 1 << stage
        for combo in sorted(held, key=lambda c: c & 2 * bit):
            held[combo | bit] = move(held[combo], blk_mask(bit))
    combos = sorted(held)
    other = {c: move(held[c], (1, 1)) for c in combos}
    parts = [held[c] for c in combos] + [other[c] for c in combos]
    masks = [pieces([c], 0) for c in combos] + [pieces([c], 1) for c in combos]
    if tiled:
        weights = place(parts, n_grp, n_slices, masks)
    else:
        flat = [m for group in masks for m in group]
        slot = [[0] * n_slices for _ in range(2)]
        for c in range(2):
            for i, m in enumerate(flat):
                slot[c][m[c]] = i
        table = jnp.where(core == 0, jnp.array(slot[0]), jnp.array(slot[1]))
        weights = jnp.concatenate(parts)[table[jnp.bitwise_xor(own, jnp.arange(n_slices))]]
    return (weights.reshape(-1), master_new.reshape(-1), moment_new.reshape(-1), second_new.reshape(-1))


def solution(mesh):
    in_specs = (P("grp", "blk", None), P(AXES), P(AXES), P(AXES))
    out_specs = (P(), P(AXES), P(AXES), P(AXES))
    body = functools.partial(shards, mesh.shape["blk"], mesh.shape["grp"])
    return jax.shard_map(body, mesh=mesh, in_specs=in_specs, out_specs=out_specs, check_vma=False)
```

```python
import functools
import jax
import jax.numpy as jnp
from jax import lax
from jax.experimental import pallas as pl
from jax.experimental.pallas import tpu as pltpu
from jax.sharding import PartitionSpec as P

STEP = 8
AXES = ("blk", "grp")
F32, BF16 = jnp.float32, jnp.bfloat16


def own_slice(n_grp):
    return lax.axis_index("blk") * n_grp + lax.axis_index("grp")


def span(masks):
    out = [0]
    for m in masks:
        out += [m ^ o for o in out]
    return out


def pack_kernel(n_grp, width, masks, g_ref, *refs):
    outs, (held, sem) = refs[:-2], refs[-2:]
    core = lax.rem(lax.axis_index("grp"), 2)
    own = own_slice(n_grp)
    flat = [pair for group in masks for pair in group]

    def copy(i):
        even, odd = flat[i]
        at = jnp.bitwise_xor(own, jnp.where(core == 0, even, odd)) * width
        return pltpu.make_async_copy(g_ref.at[:, :, pl.ds(pl.multiple_of(at, width), width)], held.at[i], sem.at[i])

    for i in range(len(flat)):
        copy(i).start()
    i = 0
    for out, group in zip(outs, masks):
        for k in range(len(group)):
            copy(i).wait()
            out[k] = held[i, 0].reshape(out.shape[1:])
            i += 1


def pack(g, n_grp, width, masks):
    count = sum(len(group) for group in masks)
    rows = (width // 128, 128)
    return pl.pallas_call(
        functools.partial(pack_kernel, n_grp, width, masks),
        in_specs=[pl.BlockSpec(memory_space=pl.ANY)],
        out_specs=[pl.BlockSpec(memory_space=pltpu.VMEM)] * len(masks),
        out_shape=[pltpu.VMEM((len(group),) + rows, BF16) for group in masks],
        scratch_shapes=[pltpu.VMEM((count, 1, 1, width), BF16), pltpu.SemaphoreType.DMA((count,))],
        cost_estimate=pl.CostEstimate(flops=0, bytes_accessed=6 * count * width, transcendentals=0),
    )(g)


def place_kernel(n_grp, n_parts, *refs):
    parts, out, sem = refs[:n_parts], refs[n_parts], refs[n_parts + 1]
    core = lax.rem(lax.axis_index("grp"), 2)
    own = own_slice(n_grp)
    return parts, out, sem, core, own


def place_body(n_grp, masks, *refs):
    parts, out, sem, core, own = place_kernel(n_grp, len(masks), *refs)
    copies = []
    for part, group in zip(parts, masks):
        for k, (even, odd) in enumerate(group):
            at = jnp.bitwise_xor(own, jnp.where(core == 0, even, odd))
            copies.append(pltpu.make_async_copy(part.at[k], out.at[at], sem.at[len(copies)]))
            copies[-1].start()
    for copy in copies:
        copy.wait()


def place(parts, n_grp, n_slices, masks):
    count = sum(len(group) for group in masks)
    rows = parts[0].shape[1:]
    return pl.pallas_call(
        functools.partial(place_body, n_grp, masks),
        in_specs=[pl.BlockSpec(memory_space=pltpu.VMEM)] * len(parts),
        out_specs=pl.BlockSpec(memory_space=pl.ANY),
        out_shape=jax.ShapeDtypeStruct((n_slices,) + rows, BF16),
        scratch_shapes=[pltpu.SemaphoreType.DMA((count,))],
    )(*(pltpu.with_memory_space_constraint(part, pltpu.VMEM) for part in parts))


def shards(n_blk, n_grp, gradients, master, moment, second):
    n_slices, n_z = n_blk * n_grp, n_grp // 2
    width = master.shape[0]
    tiled = width % 2048 == 0
    rows = (width // 128, 128) if tiled else (width,)

    bits = [1 << i for i in range(n_blk.bit_length() - 1)]
    order = (bits, bits[::-1])

    def move(value, mask_of):
        pairs = [(s, s ^ mask_of[s % 2]) for s in range(n_slices)]
        return lax.ppermute(value, AXES, pairs)

    def blk_mask(combo):
        return tuple(sum(order[c][i] for i in range(len(bits)) if combo >> i & 1) * n_grp for c in range(2))

    def pieces(combos, core_mask):
        out = []
        for combo in combos:
            even, odd = blk_mask(combo)
            if core_mask:
                even, odd = odd, even
            out += [(even ^ 2 * k ^ core_mask, odd ^ 2 * k ^ core_mask) for k in range(n_z)]
        return out

    own = own_slice(n_grp)
    core = lax.rem(own, 2)

    def take(masks):
        table = jnp.where(core == 0, jnp.array([m[0] for m in masks]), jnp.array([m[1] for m in masks]))
        return gradients.reshape(n_slices, width)[jnp.bitwise_xor(own, table)]

    def packed(groups):
        if tiled:
            return pack(gradients, n_grp, width, groups)
        return [take(group) for group in groups]

    n_stage = len(bits)
    half = 1 << max(n_stage - 1, 0)
    first = [2 * i + 1 for i in range(half)][::-1] if n_stage else [0]
    rest = [2 * i for i in range(half)][::-1] if n_stage else []

    (send_a,) = packed([pieces(first, 1)])
    got_a = move(send_a, (1, 1))
    own_a, send_b = packed([pieces(first, 0), pieces(rest, 1)])
    got_b = move(send_b, (1, 1))
    (own_b,) = packed([pieces(rest, 0)])

    total = {}
    for combos, mine, got in ((first, own_a, got_a), (rest, own_b, got_b)):
        for i, combo in enumerate(combos):
            at = slice(i * n_z, (i + 1) * n_z)
            total[combo] = mine[at].astype(F32) + got[at].astype(F32)

    for stage in range(n_stage):
        bit = 1 << stage
        left = [c for c in total if not c & bit]
        for urgent in (True, False):
            for combo in [c for c in left if bool(c & 2 * bit) == urgent]:
                got = move(total[combo | bit].astype(BF16), blk_mask(bit))
                total[combo] = total[combo] + got.astype(F32)
        total = {c: total[c] for c in left}
    part = total[0]

    radix = n_z
    while radix > 1:
        step = min(radix, 4)
        radix //= step
        part = part.reshape((step, radix) + rows)
        out = part[0]
        for k in reversed(range(1, step)):
            out = out + move(part[k].astype(BF16), (2 * k * radix,) * 2).astype(F32)
        part = out
    sums = part.reshape(rows)

    master, moment, second = (v.reshape(rows) for v in (master, moment, second))
    grad = sums / n_slices
    moment_new = 0.9 * moment + 0.1 * grad
    second_new = 0.95 * second + 0.05 * grad * grad
    update = moment_new / (1.0 - 0.9**STEP) / (jnp.sqrt(second_new / (1.0 - 0.95**STEP)) + 1e-08)
    master_new = master - 0.03 * (update + 0.1 * master)
    mine = master_new.astype(BF16)[None]

    radix = 1
    while radix < n_z:
        step = min(n_z // radix, 4)
        others = {k: move(mine, (2 * k * radix,) * 2) for k in reversed(range(1, step))}
        mine = jnp.concatenate([mine] + [others[k] for k in range(1, step)])
        radix *= step

    held = {0: mine}
    for stage in reversed(range(n_stage)):
        bit = 1 << stage
        for combo in sorted(held, key=lambda c: c & 2 * bit):
            held[combo | bit] = move(held[combo], blk_mask(bit))
    combos = sorted(held)
    other = {c: move(held[c], (1, 1)) for c in combos}
    parts = [held[c] for c in combos] + [other[c] for c in combos]
    masks = [pieces([c], 0) for c in combos] + [pieces([c], 1) for c in combos]
    if tiled:
        weights = place(parts, n_grp, n_slices, masks)
    else:
        flat = [m for group in masks for m in group]
        slot = [[0] * n_slices for _ in range(2)]
        for c in range(2):
            for i, m in enumerate(flat):
                slot[c][m[c]] = i
        table = jnp.where(core == 0, jnp.array(slot[0]), jnp.array(slot[1]))
        weights = jnp.concatenate(parts)[table[jnp.bitwise_xor(own, jnp.arange(n_slices))]]
    return (weights.reshape(-1), master_new.reshape(-1), moment_new.reshape(-1), second_new.reshape(-1))


def solution(mesh):
    in_specs = (P("grp", "blk", None), P(AXES), P(AXES), P(AXES))
    out_specs = (P(), P(AXES), P(AXES), P(AXES))
    body = functools.partial(shards, mesh.shape["blk"], mesh.shape["grp"])
    return jax.shard_map(body, mesh=mesh, in_specs=in_specs, out_specs=out_specs, check_vma=False)
```

```python
import functools

import jax
import jax.numpy as jnp
from jax import lax
from jax.experimental import pallas as pl
from jax.experimental.pallas import tpu as pltpu
from jax.sharding import PartitionSpec as P


STEP = 8
AXES = ("blk", "grp")
F32, BF16 = jnp.float32, jnp.bfloat16


def own_slice(n_grp):
    return lax.axis_index("blk") * n_grp + lax.axis_index("grp")


def pack_kernel(n_grp, width, masks, g_ref, *refs):
    outs, (held, sem) = refs[:-2], refs[-2:]
    core = lax.rem(lax.axis_index("grp"), 2)
    own = own_slice(n_grp)
    flat = [pair for group in masks for pair in group]

    def copy(i):
        even, odd = flat[i]
        at = jnp.bitwise_xor(own, jnp.where(core == 0, even, odd)) * width
        return pltpu.make_async_copy(g_ref.at[:, :, pl.ds(pl.multiple_of(at, width), width)], held.at[i], sem.at[i])

    for i in range(len(flat)):
        copy(i).start()
    i = 0
    for out, group in zip(outs, masks):
        for k in range(len(group)):
            copy(i).wait()
            out[k] = held[i, 0].reshape(out.shape[1:])
            i += 1


def pack(g, n_grp, width, masks):
    count = sum(len(group) for group in masks)
    rows = (width // 128, 128)
    return pl.pallas_call(
        functools.partial(pack_kernel, n_grp, width, masks),
        in_specs=[pl.BlockSpec(memory_space=pl.ANY)],
        out_specs=[pl.BlockSpec(memory_space=pltpu.VMEM)] * len(masks),
        out_shape=[pltpu.VMEM((len(group),) + rows, BF16) for group in masks],
        scratch_shapes=[pltpu.VMEM((count, 1, 1, width), BF16), pltpu.SemaphoreType.DMA((count,))],
        cost_estimate=pl.CostEstimate(flops=0, bytes_accessed=6 * count * width, transcendentals=0),
    )(g)


def place_kernel(n_grp, masks, n_extra, started, *refs):
    parts, refs = refs[: len(masks)], refs[len(masks) :]
    extra, refs = refs[:n_extra], refs[n_extra + started :]
    out, extra_out, sem = refs[0], refs[1:-1], refs[-1]
    core = lax.rem(lax.axis_index("grp"), 2)
    own = own_slice(n_grp)
    pairs = list(zip(extra, extra_out))
    for part, group in zip(parts, masks):
        for k, (even, odd) in enumerate(group):
            pairs.append((part.at[k], out.at[jnp.bitwise_xor(own, jnp.where(core == 0, even, odd))]))
    copies = [pltpu.make_async_copy(source, target, sem.at[i]) for i, (source, target) in enumerate(pairs)]
    for copy in copies:
        copy.start()
    for copy in copies:
        copy.wait()


def place(parts, masks, n_grp, n_slices, before, extra):
    count = sum(len(group) for group in masks) + len(extra)
    in_vmem, in_place = pl.BlockSpec(memory_space=pltpu.VMEM), pl.BlockSpec(memory_space=pl.ANY)
    held = [pltpu.with_memory_space_constraint(x, pltpu.VMEM) for x in [*parts, *extra]]
    started = before is not None
    return pl.pallas_call(
        functools.partial(place_kernel, n_grp, masks, len(extra), started),
        in_specs=[in_vmem] * len(held) + [in_place] * started,
        out_specs=[in_place] * (1 + len(extra)),
        out_shape=[jax.ShapeDtypeStruct((n_slices,) + parts[0].shape[1:], BF16)] + [jax.ShapeDtypeStruct(x.shape, x.dtype) for x in extra],
        input_output_aliases={len(held): 0} if started else {},
        scratch_shapes=[pltpu.SemaphoreType.DMA((count,))],
        cost_estimate=pl.CostEstimate(flops=0, bytes_accessed=4 * sum(part.size for part in parts), transcendentals=0),
    )(*held, *([before] if started else []))


KERNELS = (((0, 1),), ((0, 0),), ((1, 1),), ((1, 0),))
RS_GROUPS = lambda n: ([n - 1], [*range(n - 1)][::-1])
AG_GROUPS = lambda n: ([*range(n // 2, n)], [*range(n // 2)])
PLACED = lambda combos, groups: ([(c, i) for i in list(groups)[1:] for c in combos] + [(0, 0)], [(c, 0) for c in combos if c])


def value(terms):
    return functools.reduce(jnp.add, [term.astype(F32) for term in terms])


def adam(n_slices, terms, state):
    master, moment, second = state
    grad = value(terms) / n_slices
    moment_new = 0.9 * moment + 0.1 * grad
    second_new = 0.95 * second + 0.05 * grad * grad
    update = moment_new / (1.0 - 0.9**STEP) / (jnp.sqrt(second_new / (1.0 - 0.95**STEP)) + 1e-08)
    master_new = master - 0.03 * (update + 0.1 * master)
    return master_new.astype(BF16), master_new, moment_new, second_new


def adam_kernel(n_slices, n_terms, *refs):
    ins, outs = refs[: n_terms + 3], refs[n_terms + 3 :]
    for ref, result in zip(outs, adam(n_slices, [ref[...] for ref in ins[:n_terms]], [ref[...] for ref in ins[n_terms:]])):
        ref[...] = result


def adam_call(n_slices, terms, state):
    ins = [pltpu.with_memory_space_constraint(x, pltpu.VMEM) for x in terms + state]
    return pl.pallas_call(
        functools.partial(adam_kernel, n_slices, len(terms)),
        in_specs=[pl.BlockSpec(memory_space=pltpu.VMEM)] * len(ins),
        out_specs=[pl.BlockSpec(memory_space=pltpu.VMEM)] * 4,
        out_shape=[pltpu.VMEM(state[0].shape, dtype) for dtype in (BF16, F32, F32, F32)],
        cost_estimate=pl.CostEstimate(flops=30 * state[0].size, bytes_accessed=0, transcendentals=state[0].size),
    )(*ins)


def shards(n_blk, n_grp, gradients, master, moment, second):
    n_slices, n_z = n_blk * n_grp, n_grp // 2
    width = master.shape[0]
    tiled = width % 2048 == 0
    rows = (width // 128, 128) if tiled else (width,)

    n_stage = n_blk.bit_length() - 1
    bits = [1 << i for i in range(n_stage)]
    order = (bits, bits[::-1])
    combos = list(range(n_blk))
    last = n_blk >> 1

    step = min(n_z, 4)
    radix = n_z // step
    groups = [g for g in RS_GROUPS(step) if g]
    zs_of = [[digit * radix + rest for digit in group for rest in range(radix)] for group in groups]
    zs = sum(zs_of, [])
    span_of = [slice(sum(map(len, zs_of[:i])), sum(map(len, zs_of[: i + 1]))) for i in range(len(groups))]

    own = own_slice(n_grp)
    core = lax.rem(own, 2)

    def move(value, mask):
        pairs = [(s, s ^ mask[s % 2]) for s in range(n_slices)]
        return lax.ppermute(value, AXES, pairs)

    def blk_mask(combo):
        return tuple(sum(order[c][i] for i in range(n_stage) if combo >> i & 1) * n_grp for c in range(2))

    def z_mask(k):
        return (2 * k, 2 * k)

    def masks_of(combos, zs, sibling):
        out = []
        for combo in combos:
            even, odd = blk_mask(combo)[:: -1 if sibling else 1]
            out += [(even ^ 2 * k ^ sibling, odd ^ 2 * k ^ sibling) for k in zs]
        return out

    def packed(parts):
        if tiled:
            return pack(gradients, n_grp, width, parts)
        out = []
        for masks in parts:
            table = jnp.where(core == 0, jnp.array([m[0] for m in masks]), jnp.array([m[1] for m in masks]))
            out.append(gradients.reshape(n_slices, width)[jnp.bitwise_xor(own, table)])
        return out

    chunks = [c for c in ([c for c in combos if c & 1][::-1], [c for c in combos if not c & 1][::-1]) if c]
    total, laid, got = {}, {}, {}
    for kernel in KERNELS:
        kernel = [(i, sibling) for i, sibling in kernel if i < len(chunks)]
        if kernel:
            laid.update(zip(kernel, packed([masks_of(chunks[i], zs, sibling) for i, sibling in kernel])))
    for i, chunk in enumerate(chunks):
        got[i] = move(laid[i, 1], (1, 1))
        for j, combo in enumerate(chunk):
            at = slice(j * n_z, (j + 1) * n_z)
            total[combo] = laid[i, 0][at].astype(F32) + got[i][at].astype(F32)

    of = range(len(groups))
    terms = {(c, i): [total[c][at]] for c in combos for i, at in enumerate(span_of)}
    for stage in range(n_stage):
        bit = 1 << stage
        left = [c for c in combos if not c & (2 * bit - 1)]
        if bit == last:
            messages = [[(0, i)] for i in of]
        else:
            first = [(c, i) for c in left[::-1] for i in of if c & 2 * bit] + [(c, 0) for c in left if not c & 2 * bit]
            messages = [first, [(c, i) for c in left for i in of if (c, i) not in first]]
        got = []
        for keys in filter(None, messages):
            sent = jnp.concatenate([value(terms[c | bit, i]).astype(BF16) for c, i in keys])
            got.append((keys, move(sent, blk_mask(bit))))
        for keys, one in got:
            at = 0
            for c, i in keys:
                n = len(zs_of[i])
                terms[c, i].append(one[at : at + n])
                at += n

    out, more = None, []
    for i, group in enumerate(groups):
        held = value(terms[0, i])
        sent = held.astype(BF16).reshape((len(group), radix) + rows)
        held = held.reshape(sent.shape)
        for k, digit in enumerate(group):
            if digit:
                more.append(move(sent[k], z_mask(digit * radix)))
            else:
                out = held[k]
    rest = radix
    if rest > 1:
        out, more = value([out] + more), []
    while rest > 1:
        by = min(rest, 4)
        rest //= by
        held = out.reshape((by, rest) + rows)
        out = held[0]
        for k in reversed(range(1, by)):
            out = out + move(held[k].astype(BF16), z_mask(k * rest)).astype(F32)

    state = [v.reshape(rows) for v in (master, moment, second)]
    terms = [term.reshape(rows) for term in [out] + more]
    if tiled:
        mine, master_new, moment_new, second_new = adam_call(n_slices, terms, state)
    else:
        mine, master_new, moment_new, second_new = adam(n_slices, terms, state)
    mine = mine[None]

    rest = 1
    while rest < radix:
        by = min(radix // rest, 4)
        mine = jnp.concatenate([mine] + [move(mine, z_mask(k * rest)) for k in range(1, by)])
        rest *= by
    held = [mine] + [move(mine, z_mask(k * radix)) for k in range(1, step)]
    weights, table, pieces, written = None, [], {}, (master_new, moment_new, second_new)

    groups = [g for g in AG_GROUPS(step) if g]
    zs_of = [[digit * radix + rest for digit in group for rest in range(radix)] for group in groups]
    for i in reversed(range(len(groups))):
        parts = {0: jnp.concatenate([held[d] for d in groups[i]]) if len(groups[i]) > 1 else held[groups[i][0]]}
        parts.update({combo: move(parts[0], blk_mask(combo)) for combo in combos[:0:-1]})
        for c in combos:
            pieces[c, i, 0] = parts[c]
            pieces[c, i, 1] = move(parts[c], (1, 1))
    for j, some in enumerate(PLACED(combos, range(len(groups)))):
        some = [(c, i, sibling) for c, i in some for sibling in range(2)]
        masks = [masks_of([c], zs_of[i], sibling) for c, i, sibling in some]
        if tiled and some:
            weights, *extra = place([pieces[key] for key in some], masks, n_grp, n_slices, weights, () if j else written)
            written = written if j else extra
        table += [(m, pieces[key][k]) for key, group in zip(some, masks) for k, m in enumerate(group)] if not tiled else []
    master_new, moment_new, second_new = written
    if not tiled:
        slots = [[m[c] for m, unused in table] for c in range(2)]
        index = jnp.where(core == 0, *(jnp.array([slot.index(m) for m in range(n_slices)]) for slot in slots))
        weights = jnp.stack([piece for unused, piece in table])[index[jnp.bitwise_xor(own, jnp.arange(n_slices))]]
    return (weights.reshape(-1), master_new.reshape(-1), moment_new.reshape(-1), second_new.reshape(-1))


def solution(mesh):
    in_specs = (P("grp", "blk", None), P(AXES), P(AXES), P(AXES))
    out_specs = (P(), P(AXES), P(AXES), P(AXES))
    body = functools.partial(shards, mesh.shape["blk"], mesh.shape["grp"])
    return jax.shard_map(body, mesh=mesh, in_specs=in_specs, out_specs=out_specs, check_vma=False)
```

```python
import functools
import jax
import jax.numpy as jnp
from jax import lax
from jax.experimental import pallas as pl
from jax.experimental.pallas import tpu as pltpu
from jax.sharding import PartitionSpec as P


STEP = 8
AXES = ("blk", "grp")
F32, BF16 = jnp.float32, jnp.bfloat16


def own_slice(n_grp):
    return lax.axis_index("blk") * n_grp + lax.axis_index("grp")


def pack_kernel(n_grp, width, masks, g_ref, *refs):
    outs, (held, sem) = refs[:-2], refs[-2:]
    core = lax.rem(lax.axis_index("grp"), 2)
    own = own_slice(n_grp)
    flat = [pair for group in masks for pair in group]

    def copy(i):
        even, odd = flat[i]
        at = jnp.bitwise_xor(own, jnp.where(core == 0, even, odd)) * width
        return pltpu.make_async_copy(g_ref.at[:, :, pl.ds(pl.multiple_of(at, width), width)], held.at[i], sem.at[i])

    for i in range(len(flat)):
        copy(i).start()
    i = 0
    for out, group in zip(outs, masks):
        for k in range(len(group)):
            copy(i).wait()
            out[k] = held[i, 0].reshape(out.shape[1:])
            i += 1


def pack(g, n_grp, width, masks):
    count = sum(len(group) for group in masks)
    rows = (width // 128, 128)
    return pl.pallas_call(
        functools.partial(pack_kernel, n_grp, width, masks),
        in_specs=[pl.BlockSpec(memory_space=pl.ANY)],
        out_specs=[pl.BlockSpec(memory_space=pltpu.VMEM)] * len(masks),
        out_shape=[pltpu.VMEM((len(group),) + rows, BF16) for group in masks],
        scratch_shapes=[pltpu.VMEM((count, 1, 1, width), BF16), pltpu.SemaphoreType.DMA((count,))],
        cost_estimate=pl.CostEstimate(flops=0, bytes_accessed=6 * count * width, transcendentals=0),
    )(g)


def place_kernel(n_grp, masks, n_extra, started, *refs):
    parts, refs = refs[: len(masks)], refs[len(masks) :]
    extra, refs = refs[:n_extra], refs[n_extra + started :]
    out, extra_out, sem = refs[0], refs[1:-1], refs[-1]
    core = lax.rem(lax.axis_index("grp"), 2)
    own = own_slice(n_grp)
    pairs = list(zip(extra, extra_out))
    for part, group in zip(parts, masks):
        for k, (even, odd) in enumerate(group):
            pairs.append((part.at[k], out.at[jnp.bitwise_xor(own, jnp.where(core == 0, even, odd))]))
    copies = [pltpu.make_async_copy(source, target, sem.at[i]) for i, (source, target) in enumerate(pairs)]
    for copy in copies:
        copy.start()
    for copy in copies:
        copy.wait()


def place(parts, masks, n_grp, n_slices, before, extra):
    count = sum(len(group) for group in masks) + len(extra)
    in_vmem, in_place = pl.BlockSpec(memory_space=pltpu.VMEM), pl.BlockSpec(memory_space=pl.ANY)
    held = [pltpu.with_memory_space_constraint(x, pltpu.VMEM) for x in [*parts, *extra]]
    started = before is not None
    return pl.pallas_call(
        functools.partial(place_kernel, n_grp, masks, len(extra), started),
        in_specs=[in_vmem] * len(held) + [in_place] * started,
        out_specs=[in_place] * (1 + len(extra)),
        out_shape=[jax.ShapeDtypeStruct((n_slices,) + parts[0].shape[1:], BF16)] + [jax.ShapeDtypeStruct(x.shape, x.dtype) for x in extra],
        input_output_aliases={len(held): 0} if started else {},
        scratch_shapes=[pltpu.SemaphoreType.DMA((count,))],
        cost_estimate=pl.CostEstimate(flops=0, bytes_accessed=4 * sum(part.size for part in parts), transcendentals=0),
    )(*held, *([before] if started else []))


KERNELS = (((0, 1),), ((0, 0),), ((1, 1), (1, 0)))
DIRECT = (True, True)
RS_GROUPS = lambda n: ([n - 1], [*range(n - 1)][::-1])
AG_GROUPS = lambda n: ([*range(n // 2, n)], [*range(n // 2)])
PLACED = lambda combos, groups: ([(c, i) for i in list(groups)[1:] for c in combos] + [(0, 0)], [(c, 0) for c in combos if c])


def value(terms):
    return functools.reduce(jnp.add, [term.astype(F32) for term in terms])


def adam(n_slices, terms, state):
    master, moment, second = state
    grad = value(terms) / n_slices
    moment_new = 0.9 * moment + 0.1 * grad
    second_new = 0.95 * second + 0.05 * grad * grad
    update = moment_new / (1.0 - 0.9**STEP) / (jnp.sqrt(second_new / (1.0 - 0.95**STEP)) + 1e-08)
    master_new = master - 0.03 * (update + 0.1 * master)
    return master_new.astype(BF16), master_new, moment_new, second_new


def adam_kernel(n_slices, n_terms, *refs):
    ins, outs = refs[: n_terms + 3], refs[n_terms + 3 :]
    for ref, result in zip(outs, adam(n_slices, [ref[...] for ref in ins[:n_terms]], [ref[...] for ref in ins[n_terms:]])):
        ref[...] = result


def adam_call(n_slices, terms, state):
    ins = [pltpu.with_memory_space_constraint(x, pltpu.VMEM) for x in terms + state]
    return pl.pallas_call(
        functools.partial(adam_kernel, n_slices, len(terms)),
        in_specs=[pl.BlockSpec(memory_space=pltpu.VMEM)] * len(ins),
        out_specs=[pl.BlockSpec(memory_space=pltpu.VMEM)] * 4,
        out_shape=[pltpu.VMEM(state[0].shape, dtype) for dtype in (BF16, F32, F32, F32)],
        cost_estimate=pl.CostEstimate(flops=30 * state[0].size, bytes_accessed=0, transcendentals=state[0].size),
    )(*ins)


def shards(n_blk, n_grp, gradients, master, moment, second):
    n_slices, n_z = n_blk * n_grp, n_grp // 2
    width = master.shape[0]
    tiled = width % 2048 == 0
    rows = (width // 128, 128) if tiled else (width,)

    n_stage = n_blk.bit_length() - 1
    bits = [1 << i for i in range(n_stage)]
    order = (bits, bits[::-1])
    combos = list(range(n_blk))

    step = min(n_z, 4)
    radix = n_z // step
    groups = [g for g in RS_GROUPS(step) if g]
    zs_of = [[digit * radix + rest for digit in group for rest in range(radix)] for group in groups]
    zs = sum(zs_of, [])
    span_of = [slice(sum(map(len, zs_of[:i])), sum(map(len, zs_of[: i + 1]))) for i in range(len(groups))]

    own = own_slice(n_grp)
    core = lax.rem(own, 2)

    def move(value, mask):
        pairs = [(s, s ^ mask[s % 2]) for s in range(n_slices)]
        return lax.ppermute(value, AXES, pairs)

    def blk_mask(combo):
        return tuple(sum(order[c][i] for i in range(n_stage) if combo >> i & 1) * n_grp for c in range(2))

    def z_mask(k):
        return (2 * k, 2 * k)

    def masks_of(combos, zs, sibling):
        out = []
        for combo in combos:
            even, odd = blk_mask(combo)[:: -1 if sibling else 1]
            out += [(even ^ 2 * k ^ sibling, odd ^ 2 * k ^ sibling) for k in zs]
        return out

    def packed(parts):
        if tiled:
            return pack(gradients, n_grp, width, parts)
        out = []
        for masks in parts:
            table = jnp.where(core == 0, jnp.array([m[0] for m in masks]), jnp.array([m[1] for m in masks]))
            out.append(gradients.reshape(n_slices, width)[jnp.bitwise_xor(own, table)])
        return out

    chunks = [c for c in ([c for c in combos if c & 1][::-1], [c for c in combos if not c & 1][::-1]) if c]
    total, laid, got = {}, {}, {}
    for kernel in KERNELS:
        kernel = [(i, sibling) for i, sibling in kernel if i < len(chunks)]
        if kernel:
            laid.update(zip(kernel, packed([masks_of(chunks[i], zs, sibling) for i, sibling in kernel])))
    for i, chunk in enumerate(chunks):
        got[i] = move(laid[i, 1], (1, 1))
        for j, combo in enumerate(chunk):
            at = slice(j * n_z, (j + 1) * n_z)
            total[combo] = laid[i, 0][at].astype(F32) + got[i][at].astype(F32)

    out, more = None, []
    for i, (group, at) in enumerate(zip(groups, span_of)):
        terms = {c: [total[c][at]] for c in combos}
        for stage in range(n_stage):
            bit = 1 << stage
            left = [c for c in terms if not c & bit]
            sent = jnp.concatenate([value(terms[c | bit]).astype(BF16) for c in left])
            got = move(sent, blk_mask(bit))
            n = len(zs_of[i])
            terms = {c: terms[c] + [got[k * n : (k + 1) * n]] for k, c in enumerate(left)}
        held = value(terms[0])
        sent = held.astype(BF16).reshape((len(group), radix) + rows)
        held = held.reshape(sent.shape)
        for k, digit in enumerate(group):
            if digit:
                more.append(move(sent[k], z_mask(digit * radix)))
            else:
                out = held[k]
    rest = radix
    if rest > 1:
        out, more = value([out] + more), []
    while rest > 1:
        by = min(rest, 4)
        rest //= by
        held = out.reshape((by, rest) + rows)
        out = held[0]
        for k in reversed(range(1, by)):
            out = out + move(held[k].astype(BF16), z_mask(k * rest)).astype(F32)

    state = [v.reshape(rows) for v in (master, moment, second)]
    terms = [term.reshape(rows) for term in [out] + more]
    if tiled:
        mine, master_new, moment_new, second_new = adam_call(n_slices, terms, state)
    else:
        mine, master_new, moment_new, second_new = adam(n_slices, terms, state)
    mine = mine[None]

    rest = 1
    while rest < radix:
        by = min(radix // rest, 4)
        mine = jnp.concatenate([mine] + [move(mine, z_mask(k * rest)) for k in range(1, by)])
        rest *= by
    held = [mine] + [move(mine, z_mask(k * radix)) for k in range(1, step)]
    weights, table, pieces, written = None, [], {}, (master_new, moment_new, second_new)

    groups = [g for g in AG_GROUPS(step) if g]
    zs_of = [[digit * radix + rest for digit in group for rest in range(radix)] for group in groups]
    for i in reversed(range(len(groups))):
        parts = {0: jnp.concatenate([held[d] for d in groups[i]]) if len(groups[i]) > 1 else held[groups[i][0]]}
        if DIRECT[i]:
            parts.update({combo: move(parts[0], blk_mask(combo)) for combo in combos[:0:-1]})
        for stage in reversed(range(0 if DIRECT[i] else n_stage)):
            bit = 1 << stage
            for combo in sorted(parts, key=lambda c: c & 2 * bit):
                parts[combo | bit] = move(parts[combo], blk_mask(bit))
        for c in combos:
            pieces[c, i, 0] = parts[c]
            pieces[c, i, 1] = move(parts[c], (1, 1))
    for j, some in enumerate(PLACED(combos, range(len(groups)))):
        some = [(c, i, sibling) for c, i in some for sibling in range(2)]
        masks = [masks_of([c], zs_of[i], sibling) for c, i, sibling in some]
        if tiled and some:
            weights, *extra = place([pieces[key] for key in some], masks, n_grp, n_slices, weights, () if j else written)
            written = written if j else extra
        table += [(m, pieces[key][k]) for key, group in zip(some, masks) for k, m in enumerate(group)] if not tiled else []
    master_new, moment_new, second_new = written
    if not tiled:
        slots = [[m[c] for m, unused in table] for c in range(2)]
        index = jnp.where(core == 0, *(jnp.array([slot.index(m) for m in range(n_slices)]) for slot in slots))
        weights = jnp.stack([piece for unused, piece in table])[index[jnp.bitwise_xor(own, jnp.arange(n_slices))]]
    return (weights.reshape(-1), master_new.reshape(-1), moment_new.reshape(-1), second_new.reshape(-1))


def solution(mesh):
    in_specs = (P("grp", "blk", None), P(AXES), P(AXES), P(AXES))
    out_specs = (P(), P(AXES), P(AXES), P(AXES))
    body = functools.partial(shards, mesh.shape["blk"], mesh.shape["grp"])
    return jax.shard_map(body, mesh=mesh, in_specs=in_specs, out_specs=out_specs, check_vma=False)
```
